1024 devices in a mesh: head: 32 (over y_lo, x, core), seq: 32 (over z, y_hi).
Axes of the slice: x: 4, y: 8 (y_hi: 2, y_lo: 4; y = y_hi * 4 + y_lo), z: 16, core: 2. Of those that a mesh axis runs over, the one named last changes fastest.
Arguments:
- q_nope: bfloat16 [4096, 16384], P(('seq', 'head')), may hold values from -6 to 6
- q_rope: bfloat16 [4096, 8192], P(('seq', 'head')), may hold values from -512 to 512
- kv_cache: bfloat16 [4096, 576], P(('seq', 'head')), may hold values from -8 to 8
- w_key: bfloat16 [512, 16384], P(None, 'head'), may hold values from -0.25 to 0.25
- w_value: bfloat16 [512, 16384], P(None, 'head'), may hold values from -0.25 to 0.25
- dout: bfloat16 [4096, 16384], P(('seq', 'head')), may hold values from -0.8984375 to 0.8984375
- starts: int32 [32], P('seq'), may hold values from 0 to 128
Outputs:
- grad_q_nope: bfloat16 [4096, 16384], P('seq', 'head')
- grad_q_rope: bfloat16 [4096, 8192], P('seq', 'head')
- grad_kv: bfloat16 [4096, 576], P(('seq', 'head'))
The draws below stay inside these ranges and needn't reach their ends.
All inputs are finite; a program needn't handle non-finite values.
Results may differ from the reference program's by a relative error of at most 0.04.
Values may be sent and summed in bfloat16 or wider, within the bound.
No kernel may reach another device: no remote copies, remote signals or barrier semaphores. Data moves between devices by JAX's collectives and lax.ppermute only.
A program may use at most 32 MiB of HBM per device.

```python
import jax
import jax.numpy as jnp
from jax import lax

HEADS = 128
LATENT = 512
NOPE = 128
ROPE = 64
VDIM = 128
SPAN = 128
SEQ_SHARDS = 32
TOKENS = 4096


def draw_kv_cache(key, part):
    values = jax.random.normal(jax.random.fold_in(key, 4), (TOKENS, LATENT + ROPE), jnp.float32)
    return jnp.clip(values, -6.0, 6.0).astype(jnp.bfloat16)


def draw_q_rope(key, part):
    values = jax.random.normal(jax.random.fold_in(key, 5), (TOKENS, HEADS * ROPE), jnp.float32)
    return jnp.clip(values, -6.0, 6.0).astype(jnp.bfloat16)


def plant(entries, key, smallest, top_value):
    dims = entries.shape
    index_at = [jax.random.randint(jax.random.fold_in(key, axis), (), 0, dims[axis]) for axis in range(len(dims))]
    entries = entries.at[tuple(index_at)].set(smallest)
    longest = dims.index(max(dims))
    index_at[longest] = (index_at[longest] + 1) % dims[longest]
    return entries.at[tuple(index_at)].set(top_value)


def block_scale(key, extent, cuts, least, largest):
    factor_of, own = 1.0, jax.random.fold_in(key, 6)
    for dim, shards_of in cuts:
        steps = jnp.exp(jax.random.uniform(jax.random.fold_in(own, dim), (shards_of,), jnp.float32, least / len(cuts), largest / len(cuts)))
        factor_of = factor_of * jnp.repeat(steps, extent[dim] // shards_of).reshape([-1 if axis == dim else 1 for axis in range(len(extent))])
    return factor_of


def noise(own_key, dims, scale, reach, split=(), held_as=jnp.bfloat16):
    result = scale * jax.random.normal(own_key, dims, jnp.float32)
    if split:
        result = result * block_scale(own_key, dims, split, -0.22, 0.18)
    return jnp.clip(result, -reach, reach).astype(held_as)


def setup_inputs(seed: int = 0) -> dict:
    streams_of = jax.random.split(jax.random.key(seed), 8)
    return {
        "q_nope": noise(streams_of[0], (TOKENS, HEADS * NOPE), 1.0, 6.0, ((0, 1024),)),
        "q_rope": draw_q_rope(jax.random.fold_in(streams_of[7], 71), 0),
        "kv_cache": draw_kv_cache(jax.random.fold_in(streams_of[7], 71), 0),
        "w_key": noise(streams_of[3], (LATENT, HEADS * NOPE), LATENT ** -0.5, 0.25, ((1, 32),)),
        "w_value": noise(streams_of[4], (LATENT, HEADS * VDIM), LATENT ** -0.5, 0.25, ((1, 32),)),
        "dout": noise(streams_of[5], (TOKENS, HEADS * VDIM), 0.15, 0.8984375, ((0, 1024),)),
        "starts": plant(jax.random.randint(streams_of[6], (SEQ_SHARDS,), 0, SPAN + 1), jax.random.fold_in(streams_of[6], 1), 0, SPAN).astype(jnp.int32),
    }


def attend(query_nope, query_rope, grad_out, key_nope, values, key_rope, visible):
    rows = query_nope.shape[0]
    keys = key_nope.shape[0]
    heads = key_nope.shape[1] // NOPE
    score_scale = (NOPE + ROPE) ** -0.5
    query_heads = query_nope.astype(jnp.float32).reshape(rows, heads, NOPE)
    rope_heads = query_rope.astype(jnp.float32).reshape(rows, heads, ROPE)
    grad_heads = grad_out.astype(jnp.float32).reshape(rows, heads, VDIM)
    key_heads = key_nope.astype(jnp.float32).reshape(keys, heads, NOPE)
    value_heads = values.astype(jnp.float32).reshape(keys, heads, VDIM)
    rope_keys = key_rope.astype(jnp.float32)
    scores = jnp.einsum("qhd,khd->hqk", query_heads, key_heads) + jnp.einsum("qhd,kd->hqk", rope_heads, rope_keys)
    scores = jnp.where(visible[None], scores * score_scale, -jnp.inf)
    peak = jnp.max(scores, axis=-1, keepdims=True)
    weights = jnp.exp(scores - peak)
    probs = weights / jnp.sum(weights, axis=-1, keepdims=True)
    probs_low = probs.astype(jnp.bfloat16).astype(jnp.float32)
    value_grad = jnp.einsum("hqk,qhd->khd", probs_low, grad_heads).astype(jnp.bfloat16)
    grad_probs = jnp.einsum("qhd,khd->hqk", grad_heads, value_heads)
    row_delta = jnp.sum(probs * grad_probs, axis=-1, keepdims=True)
    grad_scores = (probs * (grad_probs - row_delta) * score_scale).astype(jnp.bfloat16).astype(jnp.float32)
    grad_query = jnp.einsum("hqk,khd->qhd", grad_scores, key_heads).astype(jnp.bfloat16).reshape(rows, heads * NOPE)
    grad_query_rope = jnp.einsum("hqk,kd->qhd", grad_scores, rope_keys).astype(jnp.bfloat16).reshape(rows, heads * ROPE)
    key_grad = jnp.einsum("hqk,qhd->khd", grad_scores, query_heads).astype(jnp.bfloat16).reshape(keys, heads * NOPE)
    rope_grad = jnp.einsum("hqk,qhd->kd", grad_scores, rope_heads)
    return grad_query, grad_query_rope, key_grad, value_grad.reshape(keys, heads * VDIM), rope_grad


def reference(q_nope, q_rope, kv_cache, w_key, w_value, dout, starts):
    def span_grads(index):
        begin = index * SPAN
        prior = jnp.maximum(index - 1, 0) * SPAN
        query_nope = lax.dynamic_slice_in_dim(q_nope, begin, SPAN, 0)
        query_rope = lax.dynamic_slice_in_dim(q_rope, begin, SPAN, 0)
        grad_out = lax.dynamic_slice_in_dim(dout, begin, SPAN, 0)
        own_rows = lax.dynamic_slice_in_dim(kv_cache, begin, SPAN, 0)
        prior_rows = lax.dynamic_slice_in_dim(kv_cache, prior, SPAN, 0)
        latent_rows = jnp.concatenate([own_rows, prior_rows], 0)
        latent = latent_rows[:, :LATENT]
        key_nope = jnp.dot(latent, w_key, preferred_element_type=jnp.float32).astype(jnp.bfloat16)
        values = jnp.dot(latent, w_value, preferred_element_type=jnp.float32).astype(jnp.bfloat16)
        key_rope = latent_rows[:, LATENT:]
        row_pos = jnp.arange(SPAN, dtype=jnp.int32)[:, None]
        col_pos = jnp.arange(SPAN, dtype=jnp.int32)[None, :]
        own_visible = col_pos <= row_pos
        prior_visible = (col_pos >= starts[index]) & (index > 0) & (row_pos >= 0)
        visible = jnp.concatenate([own_visible, prior_visible], 1)
        grad_query, grad_query_rope, key_grad, value_grad, rope_grad = attend(
            query_nope, query_rope, grad_out, key_nope, values, key_rope, visible)
        latent_term = jnp.dot(key_grad, w_key.T, preferred_element_type=jnp.float32)
        latent_term = latent_term + jnp.dot(value_grad, w_value.T, preferred_element_type=jnp.float32)
        term = jnp.concatenate([latent_term, rope_grad], 1)
        return grad_query, grad_query_rope, term[:SPAN], term[SPAN:]

    indices = jnp.arange(SEQ_SHARDS, dtype=jnp.int32)
    grad_query, grad_query_rope, own_term, prior_term = lax.map(span_grads, indices)
    next_prior = jnp.concatenate([prior_term[1:], jnp.zeros_like(prior_term[:1])], 0)
    total = (own_term + next_prior).reshape(TOKENS, LATENT + ROPE).astype(jnp.bfloat16)
    return (grad_query.reshape(TOKENS, HEADS * NOPE), grad_query_rope.reshape(TOKENS, HEADS * ROPE), total)
```

```python
import functools

import jax
import jax.numpy as jnp
from jax import lax
from jax.experimental import pallas as pl
from jax.experimental.pallas import tpu as pltpu
from jax.sharding import Mesh, PartitionSpec as P

LATENT = 512
NOPE = 128
ROPE = 64
VDIM = 128
LOG2E = 1.4426950408889634


def dot(a, b, contract):
    return lax.dot_general(a, b, ((contract[:1], contract[1:]), ((), ())), preferred_element_type=jnp.float32)


def pack_early_kernel(groups, *refs):
    sources, out_ref, targets, sems = refs[:4], refs[4], refs[5:9], refs[9]
    kv_ref = targets[3]
    copies = [pltpu.make_async_copy(source, target, sems.at[i]) for i, (source, target) in enumerate(zip(sources, targets))]
    for copy in copies:
        copy.start()
    copies[3].wait()
    rope = kv_ref[:, LATENT:]
    early = jnp.concatenate([rope, rope, kv_ref[:, :LATENT]], 1)
    at = 2 * (LATENT + ROPE)
    for g in range(groups):
        out_ref[g, :, LATENT:at] = early
    for copy, ref in zip(copies[:3], targets[:3]):
        copy.wait()
        width = ref.shape[1] // groups
        for g in range(groups):
            out_ref[g, :, at : at + width] = ref[:, g * width : (g + 1) * width]
        at += width


def load_weights_kernel(w_key_hbm, w_value_hbm, _, w_key_ref, w_value_ref, sems):
    copies = [
        pltpu.make_async_copy(w_key_hbm, w_key_ref, sems.at[0]),
        pltpu.make_async_copy(w_value_hbm, w_value_ref, sems.at[1]),
    ]
    for copy in copies:
        copy.start()
    for copy in copies:
        copy.wait()


VMEM = pl.BlockSpec(memory_space=pltpu.VMEM)


def pack_early(nope, grad, rope, kv, groups):
    shard = nope.shape[0]
    width = (nope.shape[1] + grad.shape[1] + rope.shape[1]) // groups + 2 * (LATENT + ROPE)
    return pl.pallas_call(
        functools.partial(pack_early_kernel, groups),
        out_shape=jax.ShapeDtypeStruct((groups, shard, width), nope.dtype),
        in_specs=[pl.BlockSpec(memory_space=pltpu.HBM)] * 4,
        out_specs=VMEM,
        scratch_shapes=[pltpu.VMEM(x.shape, x.dtype) for x in (nope, grad, rope, kv)] + [pltpu.SemaphoreType.DMA((4,))],
        name="pack_early",
        cost_estimate=pl.CostEstimate(flops=0, bytes_accessed=2 << 20, transcendentals=0),
    )(nope, grad, rope, kv)


def load_weights(w_key, w_value, after):
    return pl.pallas_call(
        load_weights_kernel,
        out_shape=(jax.ShapeDtypeStruct(w_key.shape, w_key.dtype), jax.ShapeDtypeStruct(w_value.shape, w_value.dtype)),
        in_specs=[pl.BlockSpec(memory_space=pltpu.HBM)] * 3,
        out_specs=(VMEM, VMEM),
        scratch_shapes=[pltpu.SemaphoreType.DMA((2,))],
        name="load_weights",
        compiler_params=pltpu.CompilerParams(vmem_limit_bytes=8 << 20),
        cost_estimate=pl.CostEstimate(flops=0, bytes_accessed=2 << 20, transcendentals=0),
    )(w_key, w_value, after)


def send_rows(grads, rope, w_key_ref, w_value_ref, out_ref):
    key_grad, value_grad = grads
    half = key_grad.shape[0] // 2
    term = dot(key_grad, w_key_ref[...], (1, 1)) + dot(value_grad, w_value_ref[...], (1, 1))
    term = term.astype(out_ref.dtype)
    out_ref[:, :LATENT] = term[:half]
    out_ref[:, LATENT : 2 * LATENT] = term[half:]
    out_ref[:, 2 * LATENT :] = jnp.concatenate([rope[:half], rope[half:]], 1).astype(out_ref.dtype)


def attend_kernel(
    shard, scalars_ref, q_ref, kv_ref, w_key_ref, w_value_ref,
    give_ref, score_grad_ref, keys_ref, key_grad_ref, value_grad_ref, rope_ref, bias_ref,
):
    rows = q_ref.shape[0]
    half = rows // 2
    heads = w_key_ref.shape[1] // NOPE
    scale = (NOPE + ROPE) ** (-0.5)
    bf16 = jnp.bfloat16
    grad_at = heads * NOPE
    rope_at = grad_at + heads * VDIM
    latent = jnp.concatenate([kv_ref[:, LATENT + 2 * ROPE :], kv_ref[:, :LATENT]], 0)
    key_rope = jnp.concatenate([kv_ref[:, LATENT + ROPE : LATENT + 2 * ROPE], kv_ref[:, LATENT : LATENT + ROPE]], 0)
    keys = dot(latent, w_key_ref[...], (1, 0)).astype(bf16)
    values = dot(latent, w_value_ref[...], (1, 0)).astype(bf16)
    keys_ref[...] = keys
    row = lax.broadcasted_iota(jnp.int32, (2 * rows, rows), 0)
    query_row = lax.broadcasted_iota(jnp.int32, (2 * rows, rows), 1)
    inner = row & (half - 1)
    key_row = (inner // shard) * (2 * shard) + ((row & half) // half) * shard + (inner & (shard - 1))
    visible = ((row < rows) & (key_row <= query_row)) | ((row >= rows) & ((key_row ^ half) >= scalars_ref[0]))
    bias_ref[...] = jnp.where(visible, 0.0, -jnp.inf)

    def operands(h):
        query = jnp.concatenate(
            [q_ref[:, h * NOPE : (h + 1) * NOPE], q_ref[:, rope_at + h * ROPE : rope_at + (h + 1) * ROPE]], 1
        )
        grad_out = q_ref[:, grad_at + h * VDIM : grad_at + (h + 1) * VDIM]
        return query, grad_out

    def score(h):
        query, grad_out = operands(h)
        key = jnp.concatenate([keys[:, h * NOPE : (h + 1) * NOPE], key_rope], 1)
        return dot(key, query, (1, 1)), dot(values[:, h * VDIM : (h + 1) * VDIM], grad_out, (1, 1))

    def soften(scores, grad_probs):
        scores = scores + bias_ref[...]
        weights = jnp.exp2((scores - jnp.max(scores, axis=0, keepdims=True)) * (scale * LOG2E))
        probs = weights * (1.0 / jnp.sum(weights, axis=0, keepdims=True))
        delta = jnp.sum(probs * grad_probs, axis=0, keepdims=True)
        return probs.astype(bf16), (probs * (grad_probs - delta) * scale).astype(bf16)

    def gradients(h, probs, grad_scores):
        query, grad_out = operands(h)
        score_grad_ref[h] = grad_scores
        value_grad = dot(probs, grad_out, (1, 0)).astype(bf16)
        key_grad = dot(grad_scores, query, (1, 0))
        for core in range(2):
            for part in range(2):
                put, take = slice(part * half, (part + 1) * half), slice(part * rows + core * half, part * rows + (core + 1) * half)
                key_grad_ref[core, put, h * NOPE : (h + 1) * NOPE] = key_grad[take, :NOPE].astype(bf16)
                value_grad_ref[core, put, h * VDIM : (h + 1) * VDIM] = value_grad[take]
        return key_grad[:, NOPE:]

    scored, softened, rope_grads = {}, {}, []
    for step in range(heads + 2):
        if step < heads:
            scored[step] = score(step)
        if 0 <= step - 1 < heads:
            softened[step - 1] = soften(*scored[step - 1])
        if 0 <= step - 2 < heads:
            rope_grads.append(gradients(step - 2, *softened[step - 2]))
    rope_sum = sum(rope_grads)
    for core in range(2):
        for part in range(2):
            start = part * rows + core * half
            rope_ref[core, part * half : (part + 1) * half] = rope_sum[start : start + half]
    other = 1 - scalars_ref[1]
    send_rows((key_grad_ref[other], value_grad_ref[other]), rope_ref[other], w_key_ref, w_value_ref, give_ref)


def finish_kernel(
    scalars_ref, score_grad_ref, keys_ref, key_grad_ref, value_grad_ref, rope_ref, kv_ref, w_key_ref, w_value_ref,
    keep_ref, grad_nope_ref, grad_rope_ref,
):
    core = scalars_ref[1]
    key_rope = jnp.concatenate([kv_ref[:, LATENT + ROPE : LATENT + 2 * ROPE], kv_ref[:, LATENT : LATENT + ROPE]], 0)
    send_rows((key_grad_ref[core], value_grad_ref[core]), rope_ref[core], w_key_ref, w_value_ref, keep_ref)
    for h in range(score_grad_ref.shape[0]):
        key = jnp.concatenate([keys_ref[:, h * NOPE : (h + 1) * NOPE], key_rope], 1)
        grad_query = dot(score_grad_ref[h], key, (0, 0)).astype(grad_nope_ref.dtype)
        grad_nope_ref[:, h * NOPE : (h + 1) * NOPE] = grad_query[:, :NOPE]
        grad_rope_ref[:, h * ROPE : (h + 1) * ROPE] = grad_query[:, NOPE:]


SCALARS = pl.BlockSpec(memory_space=pltpu.SMEM)


def attend(scalars, queries, latents, w_key, w_value, shard):
    rows, width = latents.shape
    heads = w_key.shape[1] // NOPE
    bf16 = jnp.bfloat16
    shape = jax.ShapeDtypeStruct
    give, *state = pl.pallas_call(
        functools.partial(attend_kernel, shard),
        out_shape=(
            shape((rows // 2, width), bf16),
            shape((heads, 2 * rows, rows), bf16),
            shape((2 * rows, heads * NOPE), bf16),
            shape((2, rows, heads * NOPE), bf16),
            shape((2, rows, heads * VDIM), bf16),
            shape((2, rows, ROPE), jnp.float32),
        ),
        in_specs=[SCALARS] + [VMEM] * 4,
        out_specs=(VMEM,) * 6,
        scratch_shapes=[pltpu.VMEM((2 * rows, rows), jnp.float32)],
        name="attend",
        compiler_params=pltpu.CompilerParams(
            vmem_limit_bytes=16 << 20
        ),
    )(scalars, queries, latents, w_key, w_value)
    keep, grad_nope, grad_rope = pl.pallas_call(
        finish_kernel,
        out_shape=(
            shape((rows // 2, width), bf16),
            shape((rows, heads * NOPE), bf16),
            shape((rows, heads * ROPE), bf16),
        ),
        in_specs=[SCALARS] + [VMEM] * 8,
        out_specs=(VMEM,) * 3,
        name="finish",
        compiler_params=pltpu.CompilerParams(vmem_limit_bytes=16 << 20),
        cost_estimate=pl.CostEstimate(flops=2 << 28, bytes_accessed=2 << 20, transcendentals=0),
    )(scalars, *state, latents, w_key, w_value)
    return give, keep, grad_nope, grad_rope


def shifted(block, distance):
    chips, spans = lax.axis_size("chip"), lax.axis_size("seq")
    route = [
        (c * spans + s, (c ^ (chips // 2)) * spans + s + distance)
        for c in range(chips)
        for s in range(spans)
        if 0 <= s + distance < spans
    ]
    return lax.ppermute(block, ("chip", "seq"), route)


def add_up_kernel(terms_ref, own_ref, prior_ref):
    total = terms_ref[0].astype(jnp.float32)
    for i in range(1, terms_ref.shape[0]):
        total = total + terms_ref[i].astype(jnp.float32)
    rope = total[:, 2 * LATENT :]
    own_ref[...] = jnp.concatenate([total[:, :LATENT], rope[:, :ROPE]], 1)
    prior_ref[...] = jnp.concatenate([total[:, LATENT : 2 * LATENT], rope[:, ROPE:]], 1)


def add_up(terms):
    shape = jax.ShapeDtypeStruct((terms.shape[1], LATENT + ROPE), jnp.float32)
    return pl.pallas_call(
        add_up_kernel,
        out_shape=(shape, shape),
        in_specs=[VMEM],
        out_specs=(VMEM, VMEM),
        name="add_up",
        compiler_params=pltpu.CompilerParams(vmem_limit_bytes=4 << 20),
    )(terms)


def per_device(q_nope, q_rope, kv_cache, w_key, w_value, dout, starts):
    chips = lax.axis_size("chip")
    groups = 2 * chips
    shard = kv_cache.shape[0]
    rows = shard * groups
    prior_cache = shifted(kv_cache, 1)

    packed = pack_early(q_nope, dout, q_rope, kv_cache, groups)
    prior_rows = jnp.broadcast_to(prior_cache[None], (groups, *prior_cache.shape))
    sent = lax.dynamic_update_slice(packed, prior_rows, (0, 0, 0))
    w_key, w_value = load_weights(w_key, w_value, sent[0, :, :128])
    received = lax.all_to_all(sent, ("chip", "core"), split_axis=0, concat_axis=0, tiled=True)
    width = 2 * (LATENT + ROPE)
    queries = received[..., width:].reshape(rows, -1)
    latents = received[..., :width].reshape(chips, 2, shard, width).swapaxes(0, 1).reshape(rows, width)
    first = jnp.where(lax.axis_index("seq") > 0, starts[0], rows)
    scalars = jnp.stack([first, lax.axis_index("core")]).astype(jnp.int32)
    give, keep, grad_nope, grad_rope = attend(scalars, queries, latents, w_key, w_value, shard)
    taken = lax.ppermute(give, "core", [(0, 1), (1, 0)])
    pair = (keep.astype(jnp.float32) + taken.astype(jnp.float32)).astype(jnp.bfloat16)
    terms = lax.all_to_all(pair.reshape(chips, shard, width), "chip", split_axis=0, concat_axis=0, tiled=True)
    own, prior = add_up(terms)
    return grad_nope, grad_rope, (own + shifted(prior, -1)).astype(jnp.bfloat16)


def solution(mesh):
    head, seq = mesh.devices.shape
    fine = Mesh(mesh.devices.reshape(head // 2, 2, seq), ("chip", "core", "seq"))
    head = ("chip", "core")
    placed = (
        P(("seq", *head), None),
        P(("seq", *head), None),
        P(("seq", *head), None),
        P(None, head),
        P(None, head),
        P(("seq", *head), None),
        P("seq"),
    )
    return jax.shard_map(
        per_device,
        mesh=fine,
        in_specs=placed,
        out_specs=(P("seq", head), P("seq", head), P(("seq", *head), None)),
        check_vma=False,
    )
```

```python
import functools

import jax
import jax.numpy as jnp
from jax import lax
from jax.experimental import pallas as pl
from jax.experimental.pallas import tpu as pltpu
from jax.sharding import Mesh, PartitionSpec as P

LATENT = 512
NOPE = 128
ROPE = 64
VDIM = 128
LOG2E = 1.4426950408889634
FIRST, LAST = 3, 3


def dot(a, b, contract):
    return lax.dot_general(a, b, ((contract[:1], contract[1:]), ((), ())), preferred_element_type=jnp.float32)


def pack_early_kernel(groups, *refs):
    sources, out_hbm, targets, parts, in_sems, out_sems = refs[:4], refs[4], refs[5:9], refs[9:13], *refs[13:]
    takes = [pltpu.make_async_copy(source, target, in_sems.at[i]) for i, (source, target) in enumerate(zip(sources, targets))]
    for take in takes:
        take.start()
    gives, at = [], LATENT + 2 * ROPE
    for i, (take, target, part) in enumerate(zip(takes, targets, parts)):
        take.wait()
        width = part.shape[2]
        for g in range(groups):
            part[g] = target[:, :LATENT] if i == 0 else target[:, g * width : (g + 1) * width]
        gives.append(pltpu.make_async_copy(part, out_hbm.at[:, :, at : at + width], out_sems.at[i]))
        gives[i].start()
        at += width
    for give in gives:
        give.wait()


def prepare_kernel(shard, scalars_ref, w_key_hbm, w_value_hbm, _, w_key_ref, w_value_ref, bias_ref, sems):
    copies = [
        pltpu.make_async_copy(w_key_hbm, w_key_ref, sems.at[0]),
        pltpu.make_async_copy(w_value_hbm, w_value_ref, sems.at[1]),
    ]
    for copy in copies:
        copy.start()
    rows = bias_ref.shape[1]
    half = rows // 2
    row = lax.broadcasted_iota(jnp.int32, bias_ref.shape, 0)
    query_row = lax.broadcasted_iota(jnp.int32, bias_ref.shape, 1)
    inner = row & (half - 1)
    key_row = (inner // shard) * (2 * shard) + ((row & half) // half) * shard + (inner & (shard - 1))
    own = (row < rows) & (key_row <= query_row)
    prior = (row >= rows) & ((key_row ^ (rows // 4 * FIRST)) >= scalars_ref[0])
    bias_ref[...] = jnp.where(own | prior, 0.0, -jnp.inf)
    for copy in copies:
        copy.wait()


VMEM = pl.BlockSpec(memory_space=pltpu.VMEM)
SCALARS = pl.BlockSpec(memory_space=pltpu.SMEM)


def pack_early(nope, grad, rope, kv, groups):
    shard = nope.shape[0]
    sources = (kv, nope, grad, rope)
    widths = [LATENT] + [x.shape[1] // groups for x in (nope, grad, rope)]
    return pl.pallas_call(
        functools.partial(pack_early_kernel, groups),
        out_shape=jax.ShapeDtypeStruct((groups, shard, LATENT + 2 * ROPE + sum(widths)), nope.dtype),
        in_specs=[pl.BlockSpec(memory_space=pltpu.HBM)] * 4,
        out_specs=pl.BlockSpec(memory_space=pltpu.HBM),
        scratch_shapes=[pltpu.VMEM(x.shape, x.dtype) for x in sources]
        + [pltpu.VMEM((groups, shard, width), nope.dtype) for width in widths]
        + [pltpu.SemaphoreType.DMA((4,))] * 2,
        name="pack_early",
        cost_estimate=pl.CostEstimate(flops=0, bytes_accessed=2 << 20, transcendentals=0),
    )(*sources)


def prepare(scalars, w_key, w_value, after, shard, rows):
    shape = jax.ShapeDtypeStruct
    return pl.pallas_call(
        functools.partial(prepare_kernel, shard),
        out_shape=(
            shape(w_key.shape, w_key.dtype),
            shape(w_value.shape, w_value.dtype),
            shape((2 * rows, rows), jnp.float32),
        ),
        in_specs=[SCALARS] + [pl.BlockSpec(memory_space=pltpu.HBM)] * 3,
        out_specs=(VMEM, VMEM, VMEM),
        scratch_shapes=[pltpu.SemaphoreType.DMA((2,))],
        name="prepare",
        compiler_params=pltpu.CompilerParams(vmem_limit_bytes=8 << 20),
        cost_estimate=pl.CostEstimate(flops=0, bytes_accessed=2 << 20, transcendentals=0),
    )(scalars, w_key, w_value, after)


def send_rows(grads, rope, w_key_ref, w_value_ref, out_ref):
    key_grad, value_grad = grads
    half = key_grad.shape[0] // 2
    term = dot(key_grad, w_key_ref[...], (1, 1)) + dot(value_grad, w_value_ref[...], (1, 1))
    term = term.astype(out_ref.dtype)
    out_ref[:, :LATENT] = term[:half]
    out_ref[:, LATENT : 2 * LATENT] = term[half:]
    out_ref[:, 2 * LATENT :] = jnp.concatenate([rope[:half], rope[half:]], 1).astype(out_ref.dtype)


def moves(rows):
    half, block = rows // 2, rows // 8
    for core in range(2):
        yield core, slice(0, half), slice(core * half, (core + 1) * half)
        for y in range(4):
            put, take = half + y * block, rows + core * half + (y ^ FIRST ^ LAST) * block
            yield core, slice(put, put + block), slice(take, take + block)


def attend_kernel(
    scalars_ref, received_ref, w_key_ref, w_value_ref, bias_ref,
    give_ref, score_grad_ref, keys_ref, key_rope_ref, key_grad_ref, value_grad_ref, rope_ref, q_ref, kv_ref,
):
    groups, shard, _ = received_ref.shape
    rows, width = kv_ref.shape
    q_ref[...] = received_ref[:, :, width:].reshape(q_ref.shape)
    by_core = received_ref[:, :, :width].reshape(groups // 2, 2, shard, width)
    for core in range(2):
        kv_ref[core * (rows // 2) : (core + 1) * (rows // 2)] = by_core[:, core].reshape(rows // 2, width)
    half = rows // 2
    heads = w_key_ref.shape[1] // NOPE
    scale = (NOPE + ROPE) ** (-0.5)
    bf16 = jnp.bfloat16
    grad_at = heads * NOPE
    rope_at = grad_at + heads * VDIM
    latent = jnp.concatenate([kv_ref[:, LATENT + 2 * ROPE :], kv_ref[:, :LATENT]], 0)
    key_rope = jnp.concatenate([kv_ref[:, LATENT + ROPE : LATENT + 2 * ROPE], kv_ref[:, LATENT : LATENT + ROPE]], 0)
    key_rope_ref[...] = key_rope
    keys = dot(latent, w_key_ref[...], (1, 0)).astype(bf16)
    values = dot(latent, w_value_ref[...], (1, 0)).astype(bf16)
    keys_ref[...] = keys
    def operands(h):
        query = jnp.concatenate(
            [q_ref[:, h * NOPE : (h + 1) * NOPE], q_ref[:, rope_at + h * ROPE : rope_at + (h + 1) * ROPE]], 1
        )
        grad_out = q_ref[:, grad_at + h * VDIM : grad_at + (h + 1) * VDIM]
        return query, grad_out

    def score(h):
        query, grad_out = operands(h)
        key = jnp.concatenate([keys[:, h * NOPE : (h + 1) * NOPE], key_rope], 1)
        return dot(key, query, (1, 1)), dot(values[:, h * VDIM : (h + 1) * VDIM], grad_out, (1, 1))

    def soften(scores, grad_probs):
        scores = scores + bias_ref[...]
        weights = jnp.exp2((scores - jnp.max(scores, axis=0, keepdims=True)) * (scale * LOG2E))
        probs = weights * (1.0 / jnp.sum(weights, axis=0, keepdims=True))
        delta = jnp.sum(probs * grad_probs, axis=0, keepdims=True)
        return probs.astype(bf16), (probs * (grad_probs - delta) * scale).astype(bf16)

    def gradients(h, probs, grad_scores):
        query, grad_out = operands(h)
        score_grad_ref[h] = grad_scores
        value_grad = dot(probs, grad_out, (1, 0)).astype(bf16)
        key_grad = dot(grad_scores, query, (1, 0))
        for core, put, take in moves(rows):
            key_grad_ref[core, put, h * NOPE : (h + 1) * NOPE] = key_grad[take, :NOPE].astype(bf16)
            value_grad_ref[core, put, h * VDIM : (h + 1) * VDIM] = value_grad[take]
        return key_grad[:, NOPE:]

    scored, softened, rope_grads = {}, {}, []
    for step in range(heads + 2):
        if step < heads:
            scored[step] = score(step)
        if 0 <= step - 1 < heads:
            softened[step - 1] = soften(*scored[step - 1])
        if 0 <= step - 2 < heads:
            rope_grads.append(gradients(step - 2, *softened[step - 2]))
    rope_sum = sum(rope_grads)
    for core, put, take in moves(rows):
        rope_ref[core, put] = rope_sum[take]
    other = 1 - scalars_ref[1]
    send_rows((key_grad_ref[other], value_grad_ref[other]), rope_ref[other], w_key_ref, w_value_ref, give_ref)


def finish_kernel(scalars_ref, key_grad_ref, value_grad_ref, rope_ref, w_key_ref, w_value_ref, keep_ref):
    core = scalars_ref[1]
    send_rows((key_grad_ref[core], value_grad_ref[core]), rope_ref[core], w_key_ref, w_value_ref, keep_ref)


def query_kernel(score_grad_ref, keys_ref, key_rope_ref, _, grad_nope_ref, grad_rope_ref):
    key_rope = key_rope_ref[...]
    for h in range(score_grad_ref.shape[0]):
        key = jnp.concatenate([keys_ref[:, h * NOPE : (h + 1) * NOPE], key_rope], 1)
        grad_query = dot(score_grad_ref[h], key, (0, 0)).astype(grad_nope_ref.dtype)
        grad_nope_ref[:, h * NOPE : (h + 1) * NOPE] = grad_query[:, :NOPE]
        grad_rope_ref[:, h * ROPE : (h + 1) * ROPE] = grad_query[:, NOPE:]


def attend(scalars, received, w_key, w_value, bias):
    groups, shard, columns = received.shape
    rows, width = groups * shard, 2 * (LATENT + ROPE)
    heads = w_key.shape[1] // NOPE
    bf16 = jnp.bfloat16
    shape = jax.ShapeDtypeStruct
    give, score_grads, keys, key_rope, *grads = pl.pallas_call(
        attend_kernel,
        out_shape=(
            shape((rows // 2, width), bf16),
            shape((heads, 2 * rows, rows), bf16),
            shape((2 * rows, heads * NOPE), bf16),
            shape((2 * rows, ROPE), bf16),
            shape((2, rows, heads * NOPE), bf16),
            shape((2, rows, heads * VDIM), bf16),
            shape((2, rows, ROPE), jnp.float32),
        ),
        in_specs=[SCALARS] + [VMEM] * 4,
        out_specs=(VMEM,) * 7,
        scratch_shapes=[
            pltpu.VMEM((rows, columns - width), bf16),
            pltpu.VMEM((rows, width), bf16),
        ],
        name="attend",
        compiler_params=pltpu.CompilerParams(
            vmem_limit_bytes=16 << 20
        ),
    )(scalars, received, w_key, w_value, bias)
    keep = pl.pallas_call(
        finish_kernel,
        out_shape=shape((rows // 2, width), bf16),
        in_specs=[SCALARS] + [VMEM] * 5,
        out_specs=VMEM,
        name="finish",
        compiler_params=pltpu.CompilerParams(vmem_limit_bytes=16 << 20),
        cost_estimate=pl.CostEstimate(flops=1 << 28, bytes_accessed=2 << 20, transcendentals=0),
    )(scalars, *grads, w_key, w_value)
    return give, keep, (score_grads, keys, key_rope)


def query_grads(state, after):
    heads, _, rows = state[0].shape
    shape = jax.ShapeDtypeStruct
    return pl.pallas_call(
        query_kernel,
        out_shape=(shape((rows, heads * NOPE), jnp.bfloat16), shape((rows, heads * ROPE), jnp.bfloat16)),
        in_specs=[VMEM] * 4,
        out_specs=(VMEM,) * 2,
        name="query_grads",
        compiler_params=pltpu.CompilerParams(vmem_limit_bytes=16 << 20),
        cost_estimate=pl.CostEstimate(flops=1 << 28, bytes_accessed=2 << 20, transcendentals=0),
    )(*state, after)


def shifted(block, distance, turn):
    chips, spans = lax.axis_size("chip"), lax.axis_size("seq")
    route = [
        (c * spans + s, (c ^ (chips // 4 * turn)) * spans + s + distance)
        for c in range(chips)
        for s in range(spans)
        if 0 <= s + distance < spans
    ]
    return lax.ppermute(block, ("chip", "seq"), route)


def add_up_kernel(terms_ref, own_ref, prior_ref):
    total = terms_ref[0].astype(jnp.float32)
    for i in range(1, terms_ref.shape[0]):
        total = total + terms_ref[i].astype(jnp.float32)
    rope = total[:, 2 * LATENT :]
    own_ref[...] = jnp.concatenate([total[:, :LATENT], rope[:, :ROPE]], 1)
    prior_ref[...] = jnp.concatenate([total[:, LATENT : 2 * LATENT], rope[:, ROPE:]], 1)


def add_up(terms):
    shape = jax.ShapeDtypeStruct((terms.shape[1], LATENT + ROPE), jnp.float32)
    return pl.pallas_call(
        add_up_kernel,
        out_shape=(shape, shape),
        in_specs=[VMEM],
        out_specs=(VMEM, VMEM),
        name="add_up",
        compiler_params=pltpu.CompilerParams(vmem_limit_bytes=4 << 20),
    )(terms)


def per_device(q_nope, q_rope, kv_cache, w_key, w_value, dout, starts):
    chips = lax.axis_size("chip")
    groups = 2 * chips
    shard = kv_cache.shape[0]
    rows = shard * groups
    prior_cache = shifted(kv_cache, 1, FIRST)

    packed = pack_early(q_nope, dout, q_rope, kv_cache, groups)
    late = jnp.concatenate([prior_cache, kv_cache[:, LATENT:]], 1)
    sent = lax.dynamic_update_slice(packed, jnp.broadcast_to(late[None], (groups, *late.shape)), (0, 0, 0))
    first = jnp.where(lax.axis_index("seq") > 0, starts[0], rows)
    scalars = jnp.stack([first, lax.axis_index("core")]).astype(jnp.int32)
    w_key, w_value, bias = prepare(scalars, w_key, w_value, sent[0, :, :128], shard, rows)
    received = lax.all_to_all(sent, ("chip", "core"), split_axis=0, concat_axis=0, tiled=True)
    width = 2 * (LATENT + ROPE)
    give, keep, state = attend(scalars, received, w_key, w_value, bias)
    taken = lax.ppermute(give, "core", [(0, 1), (1, 0)])
    pair = (keep.astype(jnp.float32) + taken.astype(jnp.float32)).astype(jnp.bfloat16)
    terms = lax.all_to_all(pair.reshape(chips, shard, width), "chip", split_axis=0, concat_axis=0, tiled=True)
    own, prior = add_up(terms)
    returned = shifted(prior, -1, LAST)
    return *query_grads(state, prior), (own + returned).astype(jnp.bfloat16)


def solution(mesh):
    head, seq = mesh.devices.shape
    fine = Mesh(mesh.devices.reshape(head // 2, 2, seq), ("chip", "core", "seq"))
    head = ("chip", "core")
    placed = (
        P(("seq", *head), None),
        P(("seq", *head), None),
        P(("seq", *head), None),
        P(None, head),
        P(None, head),
        P(("seq", *head), None),
        P("seq"),
    )
    return jax.shard_map(
        per_device,
        mesh=fine,
        in_specs=placed,
        out_specs=(P("seq", head), P("seq", head), P(("seq", *head), None)),
        check_vma=False,
    )
```
